256 devices in a mesh: row: 32 (over x_lo, z, core), col: 8 (over x_hi, y).
Axes of the slice: x: 4 (x_hi: 2, x_lo: 2; x = x_hi * 2 + x_lo), y: 4, z: 8, core: 2. Of those that a mesh axis runs over, the one named last changes fastest.
Arguments:
- features: bfloat16 [65536, 512], P(('row', 'col')), may hold values from -6 to 6
- weight: bfloat16 [512, 512], replicated, may hold values from -0.25 to 0.25
- out_grad: bfloat16 [65536, 512], P(('row', 'col')), may hold values from -6 to 6
- relu_mask: int32 [65536, 512], P(('row', 'col')), may hold values 0 or 1
- adjacency_tiles: bfloat16 [49152, 128, 128], P(('row', 'col')), may hold values from -0.1875 to 0.1875
- tile_rows: int32 [49152], P(('row', 'col')), may hold values from 0 to 15
- tile_cols: int32 [49152], P(('row', 'col')), may hold values from 0 to 63
- tile_count: int32 [256], P(('row', 'col')), may hold values from 24 to 192, as said below
Outputs:
- input_grad: bfloat16 [65536, 512], P(('row', 'col'))
- weight_grad: float32 [512, 512], replicated
The draws below stay inside these ranges and needn't reach their ends.
Inputs may be any that keep to these rules, and one draw needn't show every extreme that they name: Only the first tile_count slots of a device are live; some device has all 192 slots live in every draw.
All inputs are finite; a program needn't handle non-finite values. No bound on the sum of `relu_mask` on one device may be relied on, other than what follows from the above.
Results may differ from the reference program's by a relative error of at most 0.0049.
Values may be sent and summed in bfloat16 or wider, within the bound.
No kernel may reach another device: no remote copies, remote signals or barrier semaphores. Data moves between devices by JAX's collectives and lax.ppermute only.
A program may use at most 128 MiB of HBM per device.

```python
import math
import jax
import jax.numpy as jnp
from jax import lax

F = 512
TILE = 128
BPC = 2
TILES_DEV = 192
NODES = 65536
PANEL = 16
SLOTS = 64
TOTAL_TILES = 49152
N_COL = 8
DEVICES = 256


def draw_tile_count(key, part):
    floor_count = TILES_DEV // 8
    key_one, key_two, key_three = jax.random.split(key, 3)
    draw_one = jax.random.randint(key_one, (DEVICES,), 0, TILES_DEV - floor_count + 1)
    draw_two = jax.random.randint(key_two, (DEVICES,), 0, TILES_DEV - floor_count + 1)
    counts = floor_count + jnp.minimum(draw_one, draw_two)
    busiest = jax.random.randint(key_three, (), 0, DEVICES)
    return jnp.where(jnp.arange(DEVICES, dtype=jnp.int32) == busiest, TILES_DEV, counts).astype(jnp.int32)


def with_ends(values, own_key, least, largest):
    longest = values.shape.index(max(values.shape))
    spots = []
    for shift in (0, 1):
        where = [jax.random.randint(jax.random.fold_in(own_key, axis), (), 0, length) for axis, length in enumerate(values.shape)]
        where[longest] = (where[longest] + shift) % values.shape[longest]
        spots.append(tuple(where))
    return values.at[spots[0]].set(least).at[spots[1]].set(largest)


def steps_of(key, dims, pieces, least, largest):
    def one(dim, shards_of):
        heights = jax.random.uniform(jax.random.fold_in(jax.random.fold_in(key, 6), dim), (shards_of,), jnp.float32, least / len(pieces), largest / len(pieces))
        return jnp.repeat(jnp.exp(heights), dims[dim] // shards_of).reshape((-1,) + (1,) * (len(dims) - dim - 1))

    factor_of = one(*pieces[0])
    for cut in pieces[1:]:
        factor_of = factor_of * one(*cut)
    return factor_of


def gaussian(own_key, extent, scale, limit, cuts=(), kind=jnp.bfloat16):
    values = jax.random.normal(own_key, extent, jnp.float32) * scale
    if len(cuts) > 0:
        values = steps_of(own_key, extent, cuts, -0.22, 0.18) * values
    return jnp.clip(values, min=-limit, max=limit).astype(kind)


def setup_inputs(seed: int = 0) -> dict:
    key_of = jax.random.split(jax.random.key(seed), 9)
    features = gaussian(key_of[0], (NODES, F), 1.0, 6.0, ((0, 256),))
    weight = gaussian(key_of[1], (F, F), F ** -0.5, 0.25)
    out_grad = gaussian(key_of[2], (NODES, F), 1.0, 6.0, ((0, 256),))
    relu_mask = with_ends((jax.random.randint(key_of[3], (NODES, F), 0, 2) < 1).astype(jnp.int32), jax.random.fold_in(key_of[3], 1), 0, 1)
    adjacency_tiles = gaussian(key_of[4], (TOTAL_TILES, TILE, TILE), (1.5 * (BPC / (TILE * TILES_DEV)) ** 0.5), 0.1875, ((0, 256),))
    tile_rows = with_ends(jax.random.randint(key_of[5], (TOTAL_TILES,), 0, PANEL), jax.random.fold_in(key_of[5], 1), 0, PANEL - 1).astype(jnp.int32)
    tile_cols = with_ends(jax.random.randint(key_of[6], (TOTAL_TILES,), 0, SLOTS), jax.random.fold_in(key_of[6], 1), 0, SLOTS - 1).astype(jnp.int32)
    tile_count = draw_tile_count(jax.random.fold_in(key_of[8], 71), 0)
    return {"features": features, "weight": weight, "out_grad": out_grad, "relu_mask": relu_mask, "adjacency_tiles": adjacency_tiles, "tile_rows": tile_rows, "tile_cols": tile_cols, "tile_count": tile_count}


def reference(features, weight, out_grad, relu_mask, adjacency_tiles, tile_rows, tile_cols, tile_count):
    feature_width = features.shape[1]
    masked_grad = out_grad * relu_mask.astype(out_grad.dtype)
    grad_blocks = masked_grad.reshape(NODES // TILE, TILE, feature_width).astype(jnp.float32)
    tiles_by_device = adjacency_tiles.reshape(DEVICES, TILES_DEV, TILE, TILE)
    rows_by_device = tile_rows.reshape(DEVICES, TILES_DEV)
    cols_by_device = tile_cols.reshape(DEVICES, TILES_DEV)
    slot_ids = jnp.arange(TILES_DEV, dtype=jnp.int32)
    device_ids = jnp.arange(DEVICES, dtype=jnp.int32)

    def device_terms(running, inputs):
        device, dev_tiles, dev_rows, dev_cols, dev_count = inputs
        row_index = device // N_COL
        col_index = device % N_COL
        global_rows = row_index * PANEL + dev_rows
        global_cols = (dev_cols // BPC * N_COL + col_index) * BPC + dev_cols % BPC
        kept = jnp.where((slot_ids < dev_count)[:, None, None], dev_tiles.astype(jnp.float32), jnp.zeros((TILES_DEV, TILE, TILE), jnp.float32))
        terms = jnp.einsum('tij,tif->tjf', kept, grad_blocks[global_rows], precision=lax.Precision.HIGHEST)
        return (running.at[global_cols].add(terms), None)
    start_sum = jnp.zeros((NODES // TILE, TILE, feature_width), jnp.float32)
    node_sum = lax.scan(device_terms, start_sum, (device_ids, tiles_by_device, rows_by_device, cols_by_device, tile_count))[0]
    node_grad = node_sum.reshape(NODES, feature_width).astype(jnp.bfloat16)
    input_grad = jnp.dot(node_grad, weight.T, preferred_element_type=jnp.float32).astype(jnp.bfloat16)
    weight_grad = jnp.dot(features.T, node_grad, preferred_element_type=jnp.float32) * (1.0 / math.sqrt(NODES))
    return (input_grad, weight_grad)
```

```python
import math

import jax
import jax.numpy as jnp
from jax import lax
from jax.experimental import pallas as pl
from jax.experimental.pallas import tpu as pltpu
from jax.sharding import PartitionSpec as P


TILE = 128
N_Z, N_Y = 8, 4
SLOTS_DEV = 192
UNROLL = 8
DEPTH = 3
GROUPS = ((4,), (3, 5), (2, 6), (1, 7), (0,))


def plan_kernel(pos_ref, count_ref, rows_ref, cols_ref, codes_ref, sizes_ref):
    row, col = pos_ref[0], pos_ref[1]
    my_lo, my_z, my_core = row // 16, (row // 2) % N_Z, row % 2
    my_hi, my_y = col // N_Y, col % N_Y
    for group in range(len(GROUPS)):
        sizes_ref[group] = 0

    def place(slot, carry):
        owner_row = cols_ref[slot] // 2
        owner_lo, owner_z, owner_core = owner_row // 16, (owner_row // 2) % N_Z, owner_row % 2
        away = (owner_z - my_z + N_Z) % N_Z
        group = 4 - jnp.minimum(away, N_Z - away)
        paired = jnp.where((away == 0) | (away == 4), 1, 2)
        side = jnp.where(away > 4, 1, 0)
        far_core = jnp.where(owner_core == my_core, 0, 1)
        far_lo = jnp.where(owner_lo == my_lo, 0, 1)
        local = far_core * paired * 4 + side * 4 + far_lo * 2 + cols_ref[slot] % 2
        from_col = rows_ref[slot] // 2
        from_hi = jnp.where(from_col // N_Y == my_hi, 0, 1)
        piece = from_hi * N_Y + (my_y - from_col % N_Y + N_Y) % N_Y
        block = piece * 2 + rows_ref[slot] % 2
        size = sizes_ref[group]
        codes_ref[group * SLOTS_DEV + size] = slot + block * 256 + local * 8192
        sizes_ref[group] = size + 1
        return carry

    lax.fori_loop(0, jnp.minimum(count_ref[0], SLOTS_DEV), place, 0)


def plan(position, tile_count, tile_rows, tile_cols):
    smem = pl.BlockSpec(memory_space=pltpu.SMEM)
    return pl.pallas_call(
        plan_kernel,
        out_shape=(
            jax.ShapeDtypeStruct((len(GROUPS) * SLOTS_DEV,), jnp.int32),
            jax.ShapeDtypeStruct((8,), jnp.int32),
        ),
        in_specs=[smem] * 4,
        out_specs=(smem, smem),
        name="plan",
    )(position, tile_count, tile_rows, tile_cols)


def tile_kernel(group, codes_ref, sizes_ref, tiles_ref, *rest):
    pieces = rest[:8]
    own_ref, peer_ref, acc, panel, held, tile_sem, piece_sem = rest[8:]
    base = group * SLOTS_DEV
    size = sizes_ref[group]
    turns = (size + UNROLL - 1) // UNROLL

    def code_of(turn, lane):
        return codes_ref[base + jnp.minimum(turn * UNROLL + lane, size - 1)]

    def fetch(turn, lane):
        place = turn % DEPTH
        return pltpu.make_async_copy(
            tiles_ref.at[code_of(turn, lane) % 256], held.at[place, lane], tile_sem.at[place, lane]
        )

    piece_copies = [
        pltpu.make_async_copy(piece, panel.at[pl.ds(2 * i, 2)], piece_sem.at[i])
        for i, piece in enumerate(pieces)
    ]
    for copy in piece_copies:
        copy.start()
    for ahead in range(DEPTH - 1):

        @pl.when(ahead < turns)
        def _():
            for lane in range(UNROLL):
                fetch(ahead, lane).start()

    acc[...] = jnp.zeros_like(acc)
    for copy in piece_copies:
        copy.wait()

    def advance(turn, carry):
        @pl.when(turn + DEPTH - 1 < turns)
        def _():
            for lane in range(UNROLL):
                fetch(turn + DEPTH - 1, lane).start()

        for lane in range(UNROLL):
            fetch(turn, lane).wait()
        place = turn % DEPTH
        terms = []
        for lane in range(UNROLL):
            code = code_of(turn, lane)
            tile = held[place, lane]
            tile = jnp.where(turn * UNROLL + lane < size, tile, jnp.zeros_like(tile))
            terms.append(
                lax.dot_general(
                    tile,
                    panel[(code // 256) % 32],
                    (((0,), (0,)), ((), ())),
                    preferred_element_type=jnp.float32,
                )
            )
        for lane in range(UNROLL):
            local = code_of(turn, lane) // 8192
            acc[local] = acc[local] + terms[lane]
        return carry

    lax.fori_loop(0, turns, advance, 0)
    half = acc.shape[0] // 2
    own_ref[...] = acc[pl.ds(0, half)]
    peer_ref[...] = acc[pl.ds(half, half)].astype(jnp.bfloat16)


def tile_sums(group, codes, sizes, tiles, pieces):
    half = len(GROUPS[group]) * 4
    width = pieces[0].shape[-1]
    smem = pl.BlockSpec(memory_space=pltpu.SMEM)
    anywhere = pl.BlockSpec(memory_space=pl.ANY)
    vmem = pl.BlockSpec(memory_space=pltpu.VMEM)

    def body(*refs):
        tile_kernel(group, *refs)

    return pl.pallas_call(
        body,
        out_shape=(
            jax.ShapeDtypeStruct((half, TILE, width), jnp.float32),
            jax.ShapeDtypeStruct((half, TILE, width), jnp.bfloat16),
        ),
        in_specs=[smem, smem] + [anywhere] * 9,
        out_specs=(vmem, vmem),
        scratch_shapes=[
            pltpu.VMEM((2 * half, TILE, width), jnp.float32),
            pltpu.VMEM((16, TILE, width), jnp.bfloat16),
            pltpu.VMEM((DEPTH, UNROLL, TILE, TILE), jnp.bfloat16),
            pltpu.SemaphoreType.DMA((DEPTH, UNROLL)),
            pltpu.SemaphoreType.DMA((8,)),
        ],
        cost_estimate=pl.CostEstimate(
            flops=half * 12 * TILE * TILE * width, transcendentals=0, bytes_accessed=8 << 20
        ),
        name="tiles%d" % group,
    )(codes, sizes, tiles, *pieces)


def shift_z(x, step):
    return lax.ppermute(
        x, "row", [(i, i // 16 * 16 + (i // 2 + step) % N_Z * 2 + i % 2) for i in range(32)]
    )


def swap_core(x):
    return lax.ppermute(x, "row", [(i, i ^ 1) for i in range(32)])


def swap_lo(x):
    return lax.ppermute(x, "row", [(i, i ^ 16) for i in range(32)])


def swap_hi(x):
    return lax.ppermute(x, "col", [(i, i ^ 4) for i in range(8)])


def shift_y(x, step):
    return lax.ppermute(
        x, "col", [(i, i // N_Y * N_Y + (i + step) % N_Y) for i in range(8)]
    )


def shards(
    features, weight, out_grad, relu_mask, adjacency_tiles, tile_rows, tile_cols, tile_count
):
    width = features.shape[1]
    bf16, f32 = jnp.bfloat16, jnp.float32
    masked_grad = (out_grad * relu_mask.astype(bf16)).reshape(2, TILE, width)
    across = swap_hi(masked_grad)
    pieces = [masked_grad] + [shift_y(masked_grad, step) for step in (1, 2, 3)]
    pieces += [across] + [shift_y(across, step) for step in (1, 2, 3)]
    position = jnp.stack([lax.axis_index("row"), lax.axis_index("col")]).astype(jnp.int32)
    codes, sizes = plan(position, tile_count, tile_rows, tile_cols)

    right = left = None
    for group, away in enumerate(GROUPS):
        own, peer = tile_sums(group, codes, sizes, adjacency_tiles, pieces)
        count = len(away)
        own = own.reshape(count, 2, 2, TILE, width)
        met = swap_core(peer).reshape(count, 2, 2, TILE, width)
        far = swap_lo((own[:, 1] + met[:, 1].astype(f32)).astype(bf16))
        sums = [own[i, 0] + met[i, 0].astype(f32) + far[i].astype(f32) for i in range(count)]
        if group == 0:
            right = shift_z(sums[0][0].astype(bf16), 1)
            left = shift_z(sums[0][1].astype(bf16), -1)
        elif group == 1:
            to_right = jnp.stack([sums[0][0] + right.astype(f32), sums[0][1]])
            to_left = jnp.stack([sums[1][0], sums[1][1] + left.astype(f32)])
            right = shift_z(to_right.astype(bf16), 1)
            left = shift_z(to_left.astype(bf16), -1)
        elif group < 4:
            right = shift_z((sums[0] + right.astype(f32)).astype(bf16), 1)
            left = shift_z((sums[1] + left.astype(f32)).astype(bf16), -1)
        else:
            total = sums[0] + right.astype(f32) + left.astype(f32)
    node_grad = total.astype(bf16).reshape(-1, width)

    partial_weight = lax.dot_general(
        features, node_grad, (((0,), (0,)), ((), ())), preferred_element_type=f32
    ).astype(bf16)
    split = partial_weight.reshape(64, 8, 4, 128).transpose(0, 2, 1, 3).reshape(256, 8, 128)
    terms = lax.all_to_all(split, ("row", "col"), 0, 0)
    node_total = features.shape[0] * 256
    mine = jnp.sum(terms.astype(f32), axis=0) * (1.0 / math.sqrt(node_total))
    spread = jnp.broadcast_to(mine.astype(bf16)[None], (256, 8, 128))
    whole = lax.all_to_all(spread, ("row", "col"), 0, 0)
    weight_grad = whole.reshape(64, 4, 8, 128).transpose(0, 2, 1, 3).reshape(width, width)
    input_grad = lax.dot_general(
        node_grad, weight, (((1,), (1,)), ((), ())), preferred_element_type=f32
    ).astype(bf16)
    return (input_grad, weight_grad.astype(f32))


def solution(mesh):
    return jax.shard_map(
        shards,
        mesh=mesh,
        in_specs=(
            P(("row", "col"), None),
            P(),
            P(("row", "col"), None),
            P(("row", "col"), None),
            P(("row", "col"), None, None),
            P(("row", "col")),
            P(("row", "col")),
            P(("row", "col")),
        ),
        out_specs=(P(("row", "col"), None), P()),
        check_vma=False,
    )
```

```python
import math

import jax
import jax.numpy as jnp
from jax import lax
from jax.experimental import pallas as pl
from jax.experimental.pallas import tpu as pltpu
from jax.sharding import PartitionSpec as P


TILE = 128
N_Z, N_Y = 8, 4
SLOTS_DEV = 192
UNROLL = 8
DEPTH = 3
GROUPS = ((4,), (3, 5), (2, 6), (1, 7), (0,))


def plan_kernel(pos_ref, count_ref, rows_ref, cols_ref, codes_ref, sizes_ref):
    row, col = pos_ref[0], pos_ref[1]
    my_lo, my_z, my_core = row // 16, (row // 2) % N_Z, row % 2
    my_hi, my_y = col // N_Y, col % N_Y
    for group in range(len(GROUPS)):
        sizes_ref[group] = 0

    def place(slot, carry):
        owner_row = cols_ref[slot] // 2
        owner_lo, owner_z, owner_core = owner_row // 16, (owner_row // 2) % N_Z, owner_row % 2
        away = (owner_z - my_z + N_Z) % N_Z
        group = 4 - jnp.minimum(away, N_Z - away)
        paired = jnp.where((away == 0) | (away == 4), 1, 2)
        side = jnp.where(away > 4, 1, 0)
        far_core = jnp.where(owner_core == my_core, 0, 1)
        far_lo = jnp.where(owner_lo == my_lo, 0, 1)
        local = far_core * paired * 4 + side * 4 + far_lo * 2 + cols_ref[slot] % 2
        from_col = rows_ref[slot] // 2
        from_hi = jnp.where(from_col // N_Y == my_hi, 0, 1)
        piece = from_hi * N_Y + (my_y - from_col % N_Y + N_Y) % N_Y
        block = piece * 2 + rows_ref[slot] % 2
        size = sizes_ref[group]
        codes_ref[group * SLOTS_DEV + size] = slot + block * 256 + local * 8192
        sizes_ref[group] = size + 1
        return carry

    lax.fori_loop(0, jnp.minimum(count_ref[0], SLOTS_DEV), place, 0)


def plan(position, tile_count, tile_rows, tile_cols):
    smem = pl.BlockSpec(memory_space=pltpu.SMEM)
    return pl.pallas_call(
        plan_kernel,
        out_shape=(
            jax.ShapeDtypeStruct((len(GROUPS) * SLOTS_DEV,), jnp.int32),
            jax.ShapeDtypeStruct((8,), jnp.int32),
        ),
        in_specs=[smem] * 4,
        out_specs=(smem, smem),
        name="plan",
    )(position, tile_count, tile_rows, tile_cols)


def tile_kernel(group, codes_ref, sizes_ref, tiles_ref, *rest):
    pieces = rest[:8]
    own_ref, peer_ref, acc, panel, held, sent, tile_sem, piece_sem = rest[8:]
    base = group * SLOTS_DEV
    size = sizes_ref[group]
    turns = (size + UNROLL - 1) // UNROLL

    def code_of(turn, lane):
        return codes_ref[base + jnp.minimum(turn * UNROLL + lane, size - 1)]

    def fetch(turn, lane):
        place = turn % DEPTH
        return pltpu.make_async_copy(
            tiles_ref.at[code_of(turn, lane) % 256], held.at[place, lane], tile_sem.at[place, lane]
        )

    piece_copies = [
        pltpu.make_async_copy(piece, panel.at[pl.ds(2 * i, 2)], piece_sem.at[i])
        for i, piece in enumerate(pieces)
    ]
    for copy in piece_copies:
        copy.start()
    for ahead in range(DEPTH - 1):

        @pl.when(ahead < turns)
        def _():
            for lane in range(UNROLL):
                fetch(ahead, lane).start()

    acc[...] = jnp.zeros_like(acc)
    for copy in piece_copies:
        copy.wait()

    def advance(turn, carry):
        @pl.when(turn + DEPTH - 1 < turns)
        def _():
            for lane in range(UNROLL):
                fetch(turn + DEPTH - 1, lane).start()

        for lane in range(UNROLL):
            fetch(turn, lane).wait()
        place = turn % DEPTH
        terms = []
        for lane in range(UNROLL):
            code = code_of(turn, lane)
            tile = held[place, lane]
            tile = jnp.where(turn * UNROLL + lane < size, tile, jnp.zeros_like(tile))
            terms.append(
                lax.dot_general(
                    tile,
                    panel[(code // 256) % 32],
                    (((0,), (0,)), ((), ())),
                    preferred_element_type=jnp.float32,
                )
            )
        for lane in range(UNROLL):
            local = code_of(turn, lane) // 8192
            acc[local] = acc[local] + terms[lane]
        return carry

    lax.fori_loop(0, turns, advance, 0)
    half = acc.shape[0] // 2
    sent[...] = acc[pl.ds(half, half)].astype(jnp.bfloat16)
    peer_copy = pltpu.make_async_copy(sent, peer_ref, piece_sem.at[0])
    own_copy = pltpu.make_async_copy(acc.at[pl.ds(0, half)], own_ref, piece_sem.at[1])
    peer_copy.start()
    own_copy.start()
    peer_copy.wait()
    own_copy.wait()


def tile_sums(group, codes, sizes, tiles, pieces):
    half = len(GROUPS[group]) * 4
    width = pieces[0].shape[-1]
    smem = pl.BlockSpec(memory_space=pltpu.SMEM)
    anywhere = pl.BlockSpec(memory_space=pl.ANY)

    def body(*refs):
        tile_kernel(group, *refs)

    return pl.pallas_call(
        body,
        out_shape=(
            jax.ShapeDtypeStruct((half, TILE, width), jnp.float32),
            jax.ShapeDtypeStruct((half, TILE, width), jnp.bfloat16),
        ),
        in_specs=[smem, smem] + [anywhere] * 9,
        out_specs=(anywhere, anywhere),
        scratch_shapes=[
            pltpu.VMEM((2 * half, TILE, width), jnp.float32),
            pltpu.VMEM((16, TILE, width), jnp.bfloat16),
            pltpu.VMEM((DEPTH, UNROLL, TILE, TILE), jnp.bfloat16),
            pltpu.VMEM((half, TILE, width), jnp.bfloat16),
            pltpu.SemaphoreType.DMA((DEPTH, UNROLL)),
            pltpu.SemaphoreType.DMA((8,)),
        ],
        cost_estimate=pl.CostEstimate(
            flops=half * 12 * TILE * TILE * width, transcendentals=0, bytes_accessed=8 << 20
        ),
        name="tiles%d" % group,
    )(codes, sizes, tiles, *pieces)


def shift_z(x, step):
    return lax.ppermute(
        x, "row", [(i, i // 16 * 16 + (i // 2 + step) % N_Z * 2 + i % 2) for i in range(32)]
    )


def swap_core(x):
    return lax.ppermute(x, "row", [(i, i ^ 1) for i in range(32)])


def swap_lo(x):
    return lax.ppermute(x, "row", [(i, i ^ 16) for i in range(32)])


def swap_hi(x):
    return lax.ppermute(x, "col", [(i, i ^ 4) for i in range(8)])


def shift_y(x, step):
    return lax.ppermute(
        x, "col", [(i, i // N_Y * N_Y + (i + step) % N_Y) for i in range(8)]
    )


def shards(
    features, weight, out_grad, relu_mask, adjacency_tiles, tile_rows, tile_cols, tile_count
):
    width = features.shape[1]
    bf16, f32 = jnp.bfloat16, jnp.float32
    row, col = lax.axis_index("row"), lax.axis_index("col")
    masked_grad = (out_grad * relu_mask.astype(bf16)).reshape(2, TILE, width)
    across = swap_hi(masked_grad)
    pieces = [masked_grad] + [shift_y(masked_grad, step) for step in (1, 2, 3)]
    pieces += [across, shift_y(across, 1), swap_hi(pieces[2]), shift_y(across, 3)]
    position = jnp.stack([row, col]).astype(jnp.int32)
    codes, sizes = plan(position, tile_count, tile_rows, tile_cols)

    owns, mets, sends, fars = [], [], [], []

    def send_far(group):
        sends.append((owns[group][:, 1] + mets[group][:, 1].astype(f32)).astype(bf16))
        fars.append(swap_lo(sends[group]))

    for group, away in enumerate(GROUPS):
        if group == 1:
            codes, peer = lax.optimization_barrier((codes, peer))
        elif group > 1:
            send_far(group - 2)
            codes, sends[-1], peer = lax.optimization_barrier((codes, sends[-1], peer))
        own, peer = tile_sums(group, codes, sizes, adjacency_tiles, pieces)
        owns.append(own.reshape(len(away), 2, 2, TILE, width))
        mets.append(swap_core(peer).reshape(len(away), 2, 2, TILE, width))
    send_far(3)
    send_far(4)

    def summed(group, side):
        near = owns[group][side, 0] + mets[group][side, 0].astype(f32)
        return near + fars[group][side].astype(f32)

    start = summed(0, 0)
    right = shift_z(start[0].astype(bf16), 1).astype(f32)
    left = shift_z(start[1].astype(bf16), -1).astype(f32)
    to_right, to_left = summed(1, 0), summed(1, 1)
    right = jnp.stack([to_right[0] + right, to_right[1]])
    left = jnp.stack([to_left[0], to_left[1] + left])
    for group in (2, 3, 4):
        right = shift_z(right.astype(bf16), 1).astype(f32)
        left = shift_z(left.astype(bf16), -1).astype(f32)
        if group < 4:
            right, left = summed(group, 0) + right, summed(group, 1) + left
    total = (summed(4, 0) + right + left).reshape(-1, width)
    node_grad = total.astype(bf16)
    rest = (total - node_grad.astype(f32)).astype(bf16)

    core = row % 2
    half = width // 2

    def weight_terms(side):
        part = lax.dynamic_slice_in_dim(features, side * half, half, 1)
        return sum(
            lax.dot_general(part, x, (((0,), (0,)), ((), ())), preferred_element_type=f32)
            for x in (node_grad, rest)
        )

    met = swap_core(weight_terms(1 - core))
    mine = (weight_terms(core) + met).astype(bf16).reshape(8, -1, width)
    terms = lax.all_to_all(mine, "col", 0, 0)
    mine = jnp.sum(terms.astype(f32), axis=0).astype(bf16)
    evens = [list(range(k, 32, 2)) for k in (0, 1)]
    terms = lax.all_to_all(
        jnp.broadcast_to(mine, (16,) + mine.shape), "row", 0, 0, axis_index_groups=evens
    )
    node_total = features.shape[0] * 256
    mine = (jnp.sum(terms.astype(f32), axis=0) * (1.0 / math.sqrt(node_total))).astype(bf16)
    input_grad = sum(
        lax.dot_general(x, weight, (((1,), (1,)), ((), ())), preferred_element_type=f32)
        for x in (node_grad, rest)
    ).astype(bf16)
    mine = lax.all_to_all(jnp.broadcast_to(mine, (8,) + mine.shape), "col", 0, 0)
    mine = mine.reshape(half, width)
    met = swap_core(mine)
    first = core == 0
    weight_grad = jnp.concatenate([jnp.where(first, mine, met), jnp.where(first, met, mine)])
    return (input_grad, weight_grad.astype(f32))


def solution(mesh):
    return jax.shard_map(
        shards,
        mesh=mesh,
        in_specs=(
            P(("row", "col"), None),
            P(),
            P(("row", "col"), None),
            P(("row", "col"), None),
            P(("row", "col"), None, None),
            P(("row", "col")),
            P(("row", "col")),
            P(("row", "col")),
        ),
        out_specs=(P(("row", "col"), None), P()),
        check_vma=False,
    )
```

```python
import math

import jax
import jax.numpy as jnp
from jax import lax
from jax.experimental import pallas as pl
from jax.experimental.pallas import tpu as pltpu
from jax.sharding import PartitionSpec as P


TILE = 128
N_Z, N_Y = 8, 4
SLOTS_DEV = 192
UNROLL = 8
DEPTH = 3
GROUPS = ((4,), (3, 5), (2, 6), (1, 7), (0,))


def plan_kernel(pos_ref, count_ref, rows_ref, cols_ref, codes_ref, sizes_ref):
    row, col = pos_ref[0], pos_ref[1]
    my_lo, my_z, my_core = row // 16, (row // 2) % N_Z, row % 2
    my_hi, my_y = col // N_Y, col % N_Y
    for group in range(len(GROUPS)):
        sizes_ref[group] = 0

    def place(slot, carry):
        owner_row = cols_ref[slot] // 2
        owner_lo, owner_z, owner_core = owner_row // 16, (owner_row // 2) % N_Z, owner_row % 2
        away = (owner_z - my_z + N_Z) % N_Z
        group = 4 - jnp.minimum(away, N_Z - away)
        paired = jnp.where((away == 0) | (away == 4), 1, 2)
        side = jnp.where(away > 4, 1, 0)
        far_core = jnp.where(owner_core == my_core, 0, 1)
        far_lo = jnp.where(owner_lo == my_lo, 0, 1)
        local = far_core * paired * 4 + side * 4 + far_lo * 2 + cols_ref[slot] % 2
        from_col = rows_ref[slot] // 2
        from_hi = jnp.where(from_col // N_Y == my_hi, 0, 1)
        piece = from_hi * N_Y + (my_y - from_col % N_Y + N_Y) % N_Y
        block = piece * 2 + rows_ref[slot] % 2
        size = sizes_ref[group]
        codes_ref[group * SLOTS_DEV + size] = slot + block * 256 + local * 8192
        sizes_ref[group] = size + 1
        return carry

    lax.fori_loop(0, jnp.minimum(count_ref[0], SLOTS_DEV), place, 0)


def plan(position, tile_count, tile_rows, tile_cols):
    smem = pl.BlockSpec(memory_space=pltpu.SMEM)
    return pl.pallas_call(
        plan_kernel,
        out_shape=(
            jax.ShapeDtypeStruct((len(GROUPS) * SLOTS_DEV,), jnp.int32),
            jax.ShapeDtypeStruct((8,), jnp.int32),
        ),
        in_specs=[smem] * 4,
        out_specs=(smem, smem),
        name="plan",
    )(position, tile_count, tile_rows, tile_cols)


def tile_kernel(group, codes_ref, sizes_ref, tiles_ref, *rest):
    pieces = rest[:8]
    own_ref, peer_ref, acc, panel, held, sent, tile_sem, piece_sem = rest[8:]
    base = group * SLOTS_DEV
    size = sizes_ref[group]
    turns = (size + UNROLL - 1) // UNROLL

    def code_of(turn, lane):
        return codes_ref[base + jnp.minimum(turn * UNROLL + lane, size - 1)]

    def fetch(turn, lane):
        place = turn % DEPTH
        return pltpu.make_async_copy(
            tiles_ref.at[code_of(turn, lane) % 256], held.at[place, lane], tile_sem.at[place, lane]
        )

    piece_copies = [
        pltpu.make_async_copy(piece, panel.at[pl.ds(2 * i, 2)], piece_sem.at[i])
        for i, piece in enumerate(pieces)
    ]
    for copy in piece_copies:
        copy.start()
    for ahead in range(DEPTH - 1):

        @pl.when(ahead < turns)
        def _():
            for lane in range(UNROLL):
                fetch(ahead, lane).start()

    acc[...] = jnp.zeros_like(acc)
    for copy in piece_copies:
        copy.wait()

    def advance(turn, carry):
        @pl.when(turn + DEPTH - 1 < turns)
        def _():
            for lane in range(UNROLL):
                fetch(turn + DEPTH - 1, lane).start()

        for lane in range(UNROLL):
            fetch(turn, lane).wait()
        place = turn % DEPTH
        terms = []
        for lane in range(UNROLL):
            code = code_of(turn, lane)
            tile = held[place, lane]
            tile = jnp.where(turn * UNROLL + lane < size, tile, jnp.zeros_like(tile))
            terms.append(
                lax.dot_general(
                    tile,
                    panel[(code // 256) % 32],
                    (((0,), (0,)), ((), ())),
                    preferred_element_type=jnp.float32,
                )
            )
        for lane in range(UNROLL):
            local = code_of(turn, lane) // 8192
            acc[local] = acc[local] + terms[lane]
        return carry

    lax.fori_loop(0, turns, advance, 0)
    half = acc.shape[0] // 2
    sent[...] = acc[pl.ds(half, half)].astype(jnp.bfloat16)
    peer_copy = pltpu.make_async_copy(sent, peer_ref, piece_sem.at[0])
    own_copy = pltpu.make_async_copy(acc.at[pl.ds(0, half)], own_ref, piece_sem.at[1])
    peer_copy.start()
    own_copy.start()
    peer_copy.wait()
    own_copy.wait()


def tile_sums(group, codes, sizes, tiles, pieces):
    half = len(GROUPS[group]) * 4
    width = pieces[0].shape[-1]
    smem = pl.BlockSpec(memory_space=pltpu.SMEM)
    anywhere = pl.BlockSpec(memory_space=pl.ANY)

    def body(*refs):
        tile_kernel(group, *refs)

    return pl.pallas_call(
        body,
        out_shape=(
            jax.ShapeDtypeStruct((half, TILE, width), jnp.float32),
            jax.ShapeDtypeStruct((half, TILE, width), jnp.bfloat16),
        ),
        in_specs=[smem, smem] + [anywhere] * 9,
        out_specs=(anywhere, anywhere),
        scratch_shapes=[
            pltpu.VMEM((2 * half, TILE, width), jnp.float32),
            pltpu.VMEM((16, TILE, width), jnp.bfloat16),
            pltpu.VMEM((DEPTH, UNROLL, TILE, TILE), jnp.bfloat16),
            pltpu.VMEM((half, TILE, width), jnp.bfloat16),
            pltpu.SemaphoreType.DMA((DEPTH, UNROLL)),
            pltpu.SemaphoreType.DMA((8,)),
        ],
        cost_estimate=pl.CostEstimate(
            flops=half * 12 * TILE * TILE * width, transcendentals=0, bytes_accessed=8 << 20
        ),
        name="tiles%d" % group,
    )(codes, sizes, tiles, *pieces)


def shift_z(x, step):
    return lax.ppermute(
        x, "row", [(i, i // 16 * 16 + (i // 2 + step) % N_Z * 2 + i % 2) for i in range(32)]
    )


def swap_core(x):
    return lax.ppermute(x, "row", [(i, i ^ 1) for i in range(32)])


def swap_lo(x):
    return lax.ppermute(x, "row", [(i, i ^ 16) for i in range(32)])


def swap_hi(x):
    return lax.ppermute(x, "col", [(i, i ^ 4) for i in range(8)])


def shift_y(x, step):
    return lax.ppermute(
        x, "col", [(i, i // N_Y * N_Y + (i + step) % N_Y) for i in range(8)]
    )


def shards(
    features, weight, out_grad, relu_mask, adjacency_tiles, tile_rows, tile_cols, tile_count
):
    width = features.shape[1]
    bf16, f32 = jnp.bfloat16, jnp.float32
    row, col = lax.axis_index("row"), lax.axis_index("col")
    masked_grad = (out_grad * relu_mask.astype(bf16)).reshape(2, TILE, width)
    across = swap_hi(masked_grad)
    pieces = [masked_grad] + [shift_y(masked_grad, step) for step in (1, 2, 3)]
    pieces += [across, shift_y(across, 1), swap_hi(pieces[2]), shift_y(across, 3)]
    position = jnp.stack([row, col]).astype(jnp.int32)
    codes, sizes = plan(position, tile_count, tile_rows, tile_cols)

    owns, mets, sends, fars, peers = [], [], [], [], []

    def send_far(group):
        sends.append((owns[group][:, 1] + mets[group][:, 1].astype(f32)).astype(bf16))
        fars.append(swap_lo(sends[group]))

    for group, away in enumerate(GROUPS):
        if group == 1:
            codes, peer = lax.optimization_barrier((codes, peer))
        elif group > 1:
            send_far(group - 2)
            codes, sends[-1], peer = lax.optimization_barrier((codes, sends[-1], peer))
        own, peer = tile_sums(group, codes, sizes, adjacency_tiles, pieces)
        peers.append(peer)
        owns.append(own.reshape(len(away), 2, 2, TILE, width))
        mets.append(swap_core(peer).reshape(len(away), 2, 2, TILE, width))
    send_far(3)
    send_far(4)

    def summed(group, side):
        near = owns[group][side, 0] + mets[group][side, 0].astype(f32)
        return near + fars[group][side].astype(f32)

    start, _ = lax.optimization_barrier((summed(0, 0), peers[3]))
    right = shift_z(start[0].astype(bf16), 1).astype(f32)
    left = shift_z(start[1].astype(bf16), -1).astype(f32)
    to_right, to_left = summed(1, 0), summed(1, 1)
    right = jnp.stack([to_right[0] + right, to_right[1]])
    left = jnp.stack([to_left[0], to_left[1] + left])
    for group in (2, 3, 4):
        right = shift_z(right.astype(bf16), 1).astype(f32)
        left = shift_z(left.astype(bf16), -1).astype(f32)
        if group < 4:
            right, left = summed(group, 0) + right, summed(group, 1) + left
    total = (summed(4, 0) + right + left).reshape(-1, width)
    rounded = lax.reduce_precision(total, 8, 7)
    node_grad = rounded.astype(bf16)
    rest = (total - rounded).astype(bf16)

    core = row % 2
    half = width // 2

    def weight_terms(side):
        part = lax.dynamic_slice_in_dim(features, side * half, half, 1)
        return sum(
            lax.dot_general(part, x, (((0,), (0,)), ((), ())), preferred_element_type=f32)
            for x in (node_grad, rest)
        )

    met = swap_core(weight_terms(1 - core))
    mine = (weight_terms(core) + met).astype(bf16).reshape(8, -1, width)
    terms = lax.all_to_all(mine, "col", 0, 0)
    mine = jnp.sum(terms.astype(f32), axis=0).astype(bf16)
    evens = [list(range(k, 32, 2)) for k in (0, 1)]
    terms = lax.all_to_all(
        jnp.broadcast_to(mine, (16,) + mine.shape), "row", 0, 0, axis_index_groups=evens
    )
    node_total = features.shape[0] * 256
    mine = (jnp.sum(terms.astype(f32), axis=0) * (1.0 / math.sqrt(node_total))).astype(bf16)
    input_grad = sum(
        lax.dot_general(x, weight, (((1,), (1,)), ((), ())), preferred_element_type=f32)
        for x in (node_grad, rest)
    ).astype(bf16)
    mine = lax.all_to_all(jnp.broadcast_to(mine, (8,) + mine.shape), "col", 0, 0)
    mine = mine.reshape(half, width)
    met = swap_core(mine)
    first = core == 0
    weight_grad = jnp.concatenate([jnp.where(first, mine, met), jnp.where(first, met, mine)])
    return (input_grad, weight_grad.astype(f32))


def solution(mesh):
    return jax.shard_map(
        shards,
        mesh=mesh,
        in_specs=(
            P(("row", "col"), None),
            P(),
            P(("row", "col"), None),
            P(("row", "col"), None),
            P(("row", "col"), None, None),
            P(("row", "col")),
            P(("row", "col")),
            P(("row", "col")),
        ),
        out_specs=(P(("row", "col"), None), P()),
        check_vma=False,
    )
```
